32 devices in a mesh: pairs: 2 (over y), ctx: 8 (over z, x), head: 2 (over core).
Axes of the slice: x: 2, y: 2, z: 4, core: 2. Of those that a mesh axis runs over, the one named last changes fastest.
Arguments:
- hidden: bfloat16 [16, 2, 8192], P(('pairs', 'ctx')), parts along dimension 0, may hold values from -6 to 6
- wq: bfloat16 [8192, 4096], P('ctx', 'head'), may hold values from -0.0625 to 0.0625
- wkv: bfloat16 [2, 8192, 512], P(None, 'ctx', 'head'), may hold values from -0.0625 to 0.0625
- bias_q: bfloat16 [4096], P('head'), may hold values from -5.2 to 5.2
- bias_kv: bfloat16 [2, 512], P(None, 'head'), may hold values from -5.2 to 5.2
- key_value_cache: bfloat16 [2, 8192, 512], P(None, ('pairs', 'ctx'), 'head'), parts along dimension 1, may hold values from -46 to 46, as said below
- prompt_len: int32 [2], P('pairs'), parts along dimension 0, may hold values from 512 to 4096
- resp_len: int32 [4], P('pairs'), parts along dimension 0, may hold values from 2 to 8
Outputs:
- attn_out: bfloat16 [16, 2, 4096], P(('pairs', 'ctx'), None, 'head'), parts along dimension 0
The draws below stay inside these ranges and needn't reach their ends.
There are 2 independent parts, one for each index of `pairs`. The reference program is written for one: setup_inputs(seed, part) draws one part's arguments, and reference() takes and returns one part's arrays. A program takes and returns all parts, laid end to end along the dimension named above; an argument that names none is the same for every part. Nothing has to cross between parts.
Inputs may be any that keep to these rules, and one draw needn't show every extreme that they name: `key_value_cache`: entries beyond prompt_len are padding and must not be attended to. Prompt positions from prompt_len on are padding. Token slots of response r from resp_len[r] on are padding.
All inputs are finite; a program needn't handle non-finite values.
Results may differ from the reference program's by a relative error of at most 0.025.
Values may be sent and summed in bfloat16 or wider, within the bound.
No kernel may reach another device: no remote copies, remote signals or barrier semaphores. Data moves between devices by JAX's collectives and lax.ppermute only.
A program may use at most 64 MiB of HBM per device.

```python
import jax
import jax.numpy as jnp
from jax import lax

MODEL_WIDTH = 8192
QUERY_HEADS = 32
KEY_VALUE_HEADS = 4
HEAD_SIZE = 128
DEVICE_PROMPT = 512
RESPONSE_SLOTS = 8
PROMPT_LENGTH = 4096
N_CTX = 8


def shared_direction(key):
    return jnp.clip(jax.random.normal(jax.random.fold_in(key, 11), (KEY_VALUE_HEADS, HEAD_SIZE), jnp.float32), -4.0, 4.0)


def draw_bias_q(key, part):
    direction = shared_direction(key)
    random_perturbations = jnp.clip(jax.random.normal(jax.random.fold_in(key, 12), (KEY_VALUE_HEADS, QUERY_HEADS // KEY_VALUE_HEADS, HEAD_SIZE), jnp.float32), -4.0, 4.0)
    return (direction[:, None, :] + 0.3 * random_perturbations).reshape(QUERY_HEADS * HEAD_SIZE).astype(jnp.bfloat16)


def draw_bias_kv(key, part):
    direction = shared_direction(key)
    random_perturbations = jnp.clip(jax.random.normal(jax.random.fold_in(key, 13), (2, KEY_VALUE_HEADS, HEAD_SIZE), jnp.float32), -4.0, 4.0)
    stacked_pairs = jnp.stack((direction + 0.3 * random_perturbations[0], 0.5 * random_perturbations[1]))
    return stacked_pairs.reshape(2, KEY_VALUE_HEADS * HEAD_SIZE).astype(jnp.bfloat16)


def draw_key_value_cache(key, part):
    stored_cache_shape = (PROMPT_LENGTH, KEY_VALUE_HEADS * HEAD_SIZE)
    keys_part = 2.2 * jnp.clip(jax.random.normal(jax.random.fold_in(key, 21), stored_cache_shape, jnp.float32), -4.0, 4.0)
    values_part = jnp.clip(jax.random.normal(jax.random.fold_in(key, 22), stored_cache_shape, jnp.float32), -4.0, 4.0)
    return jnp.stack((keys_part, values_part)).astype(jnp.bfloat16)


def levels(own_key, dims, shards, low, high):
    level = 1.0
    for dim, blocks in shards:
        draws = jax.random.uniform(jax.random.fold_in(jax.random.fold_in(own_key, 6), dim), (blocks,), jnp.float32, low / len(shards), high / len(shards))
        level = level * jnp.repeat(jnp.exp(draws), dims[dim] // blocks).reshape((-1,) + (1,) * (len(dims) - 1 - dim))
    return level


def normal_values(stream_key, shape, width, most, pieces=(), kind=jnp.bfloat16):
    entries = width * jax.random.normal(stream_key, shape, jnp.float32)
    if pieces:
        entries = entries * levels(stream_key, shape, pieces, -0.22, 0.18)
    return jnp.clip(entries, -most, most).astype(kind)


def setup_inputs(seed: int = 0, part: int = 0) -> dict:
    key_of = jax.random.split(jax.random.key(seed), 9)
    part_splits = jax.random.split(jax.random.fold_in(key_of[8], part), 9)
    hidden = normal_values(part_splits[0], (RESPONSE_SLOTS, 2, MODEL_WIDTH), 1.0, 6.0, ((0, 8),))
    wq = normal_values(key_of[1], (MODEL_WIDTH, QUERY_HEADS * HEAD_SIZE), MODEL_WIDTH ** -0.5, 0.0625, ((0, 8), (1, 2)))
    wkv = normal_values(key_of[2], (2, MODEL_WIDTH, KEY_VALUE_HEADS * HEAD_SIZE), MODEL_WIDTH ** -0.5, 0.0625, ((1, 8), (2, 2)))
    bias_q = draw_bias_q(jax.random.fold_in(key_of[8], 71), part)
    bias_kv = draw_bias_kv(jax.random.fold_in(key_of[8], 71), part)
    key_value_cache = draw_key_value_cache(jax.random.fold_in(jax.random.fold_in(key_of[8], part), 71), part)
    prompt_len = jax.random.randint(part_splits[6], (1,), PROMPT_LENGTH // 8, PROMPT_LENGTH + 1).astype(jnp.int32)
    resp_len = jax.random.randint(part_splits[7], (2,), RESPONSE_SLOTS // 4, RESPONSE_SLOTS + 1).astype(jnp.int32)
    return {"hidden": hidden, "wq": wq, "wkv": wkv, "bias_q": bias_q, "bias_kv": bias_kv, "key_value_cache": key_value_cache, "prompt_len": prompt_len, "resp_len": resp_len}


NEG_FILL = -1e30


def reference(hidden, wq, wkv, bias_q, bias_kv, key_value_cache, prompt_len, resp_len):
    query_group_width = QUERY_HEADS // KEY_VALUE_HEADS
    score_scale = HEAD_SIZE ** -0.5
    highest = lax.Precision.HIGHEST
    rows = hidden.reshape(2 * RESPONSE_SLOTS, MODEL_WIDTH)
    query_vector = (jnp.dot(rows, wq, preferred_element_type=jnp.float32) + bias_q.astype(jnp.float32)).astype(jnp.bfloat16)
    response_key = (jnp.dot(rows, wkv[0], preferred_element_type=jnp.float32) + bias_kv[0].astype(jnp.float32)).astype(jnp.bfloat16)
    response_value = (jnp.dot(rows, wkv[1], preferred_element_type=jnp.float32) + bias_kv[1].astype(jnp.float32)).astype(jnp.bfloat16)
    query_rows = query_vector.astype(jnp.float32).reshape(2 * RESPONSE_SLOTS, KEY_VALUE_HEADS, query_group_width, HEAD_SIZE)
    prompt_key_rows = key_value_cache[0].reshape(N_CTX, DEVICE_PROMPT, KEY_VALUE_HEADS, HEAD_SIZE)
    prompt_value_rows = key_value_cache[1].reshape(N_CTX, DEVICE_PROMPT, KEY_VALUE_HEADS, HEAD_SIZE)
    live_limit = prompt_len[0]

    def visit(carry, inputs):
        running_max, running_sum, weighted = carry
        block_keys, block_values, block_index = inputs
        scores = jnp.einsum("rgjd,kgd->grjk", query_rows, block_keys.astype(jnp.float32), precision=highest) * score_scale
        position = block_index * DEVICE_PROMPT + jnp.arange(DEVICE_PROMPT, dtype=jnp.int32)
        is_live = position < live_limit
        scores = jnp.where(is_live, scores, NEG_FILL)
        new_max = jnp.maximum(running_max, jnp.max(scores, axis=-1))
        unscaled = jnp.where(is_live, jnp.exp(scores - new_max[..., None]), 0.0)
        factor = jnp.exp(running_max - new_max)
        running_sum = running_sum * factor + jnp.sum(unscaled, axis=-1)
        rounded = lax.optimization_barrier(unscaled.astype(jnp.bfloat16)).astype(jnp.float32)
        weighted = weighted * factor[..., None] + jnp.einsum("grjk,kgd->grjd", rounded, block_values.astype(jnp.float32), precision=highest)
        return (new_max, running_sum, weighted), None

    statistic_shape = (KEY_VALUE_HEADS, 2 * RESPONSE_SLOTS, query_group_width)
    start_state = (jnp.full(statistic_shape, NEG_FILL, jnp.float32), jnp.zeros(statistic_shape, jnp.float32), jnp.zeros(statistic_shape + (HEAD_SIZE,), jnp.float32))
    closing_state, unused = lax.scan(visit, start_state, (prompt_key_rows, prompt_value_rows, jnp.arange(N_CTX, dtype=jnp.int32)))
    prompt_running_peak = closing_state[0].reshape(KEY_VALUE_HEADS, RESPONSE_SLOTS, 2, query_group_width)
    prompt_weight_sum = closing_state[1].reshape(KEY_VALUE_HEADS, RESPONSE_SLOTS, 2, query_group_width)
    prompt_accumulator = closing_state[2].reshape(KEY_VALUE_HEADS, RESPONSE_SLOTS, 2, query_group_width, HEAD_SIZE)

    response_query = query_rows.reshape(RESPONSE_SLOTS, 2, KEY_VALUE_HEADS, query_group_width, HEAD_SIZE)
    fresh_key_rows = response_key.astype(jnp.float32).reshape(RESPONSE_SLOTS, 2, KEY_VALUE_HEADS, HEAD_SIZE)
    fresh_value_rows = response_value.astype(jnp.float32).reshape(RESPONSE_SLOTS, 2, KEY_VALUE_HEADS, HEAD_SIZE)
    self_scores = jnp.einsum("trgjd,urgd->gtrju", response_query, fresh_key_rows, precision=highest) * score_scale
    token_pos = jnp.arange(RESPONSE_SLOTS, dtype=jnp.int32)
    self_live = (token_pos[None, None, :] <= token_pos[:, None, None]) & (token_pos[None, None, :] < resp_len[None, :, None])
    self_live = self_live[None, :, :, None, :]
    self_scores = jnp.where(self_live, self_scores, NEG_FILL)
    self_max = jnp.max(self_scores, axis=-1)
    self_weights = jnp.where(self_live, jnp.exp(self_scores - self_max[..., None]), 0.0)
    self_sum = jnp.sum(self_weights, axis=-1)
    self_rounded = lax.optimization_barrier(self_weights.astype(jnp.bfloat16)).astype(jnp.float32)
    self_acc = jnp.einsum("gtrju,urgd->gtrjd", self_rounded, fresh_value_rows, precision=highest)

    overall = jnp.maximum(prompt_running_peak, self_max)
    cache_factor = jnp.exp(prompt_running_peak - overall)
    self_factor = jnp.exp(self_max - overall)
    numerator = cache_factor[..., None] * prompt_accumulator + self_factor[..., None] * self_acc
    denominator = cache_factor * prompt_weight_sum + self_factor * self_sum
    result = numerator / denominator[..., None]
    row_live = token_pos[:, None] < resp_len[None, :]
    result = jnp.where(row_live[None, :, :, None, None], result, 0.0)
    return jnp.transpose(result, (1, 2, 0, 3, 4)).reshape(RESPONSE_SLOTS, 2, QUERY_HEADS * HEAD_SIZE).astype(jnp.bfloat16)
```

```python
import jax
import jax.numpy as jnp
from jax import lax
from jax.sharding import PartitionSpec as P

HEAD_SIZE = 128
NEG_FILL = -1e30


def split_columns(rows, parts):
    width = rows.shape[1] // parts
    if parts <= 16:
        return jnp.stack([rows[:, d * width : (d + 1) * width] for d in range(parts)])
    return jnp.swapaxes(rows.reshape(rows.shape[0], parts, width), 0, 1)


def sum_over(value, axis, size):
    bit = 1
    while bit < size:
        pairs = [(d, d ^ bit) for d in range(size)]
        other = lax.ppermute(value.astype(jnp.bfloat16), axis, pairs)
        value = value + other.astype(jnp.float32)
        bit *= 2
    return value


def shards(hidden, wq, wkv, bias_q, bias_kv, key_value_cache, prompt_len, resp_len):
    tok_dev = hidden.shape[0]
    size = lax.axis_size("ctx")
    ctx_index = lax.axis_index("ctx")
    resp_tokens = tok_dev * size
    q_width = wq.shape[1]
    k_width = wkv.shape[2]
    kv_local = k_width // HEAD_SIZE
    group = q_width // k_width
    scale = HEAD_SIZE ** (-0.5)
    row_count = 2 * tok_dev
    rows = 2 * resp_tokens

    sent = split_columns(hidden.reshape(row_count, hidden.shape[2]), size)
    columns = lax.all_to_all(sent, "ctx", split_axis=0, concat_axis=0, tiled=True)
    flat_rows = columns.reshape(rows, columns.shape[2])
    partial = jnp.concatenate(
        (
            jnp.dot(flat_rows, wq, preferred_element_type=jnp.float32),
            jnp.dot(flat_rows, wkv[0], preferred_element_type=jnp.float32),
            jnp.dot(flat_rows, wkv[1], preferred_element_type=jnp.float32),
        ),
        axis=1,
    )
    bias_all = jnp.concatenate((bias_q, bias_kv[0], bias_kv[1])).astype(jnp.float32)
    projected = (sum_over(partial, "ctx", size) + bias_all).astype(jnp.bfloat16)
    query = projected[:, :q_width].reshape(rows, kv_local, group, HEAD_SIZE)

    cache_len = key_value_cache.shape[1]
    keys = key_value_cache[0].reshape(cache_len, kv_local, HEAD_SIZE)
    values = key_value_cache[1].reshape(cache_len, kv_local, HEAD_SIZE)
    live = ctx_index * cache_len + lax.iota(jnp.int32, cache_len) < prompt_len[0]
    scores = jnp.einsum("rgjd,kgd->rgjk", query, keys, preferred_element_type=jnp.float32) * scale
    scores = jnp.where(live, scores, NEG_FILL)
    peak = jnp.max(scores, axis=-1)
    weights = jnp.where(live, jnp.exp(scores - peak[..., None]), 0.0)
    total = jnp.sum(weights, axis=-1)
    acc = jnp.einsum(
        "rgjk,kgd->rgjd", weights.astype(jnp.bfloat16), values, preferred_element_type=jnp.float32
    )
    any_live = total > 0.0
    safe = jnp.where(any_live, total, 1.0)
    lse = jnp.where(any_live, peak + jnp.log(safe), NEG_FILL)
    out = acc / safe[..., None]
    packed = jnp.stack((out, jnp.broadcast_to(lse[..., None], out.shape)), axis=1)
    packed = packed.reshape((size, row_count, 2) + out.shape[1:])
    remote = lax.all_to_all(packed, "ctx", split_axis=0, concat_axis=0, tiled=True)

    owned = lax.dynamic_slice_in_dim(projected, ctx_index * row_count, row_count, 0)
    owned_q = owned[:, :q_width].reshape(tok_dev, 2, kv_local, group, HEAD_SIZE)
    fresh_keys = projected[:, q_width : q_width + k_width].reshape(
        resp_tokens, 2, kv_local, HEAD_SIZE
    )
    fresh_values = projected[:, q_width + k_width :].reshape(resp_tokens, 2, kv_local, HEAD_SIZE)
    self_scores = (
        jnp.einsum("trgjd,urgd->trgju", owned_q, fresh_keys, preferred_element_type=jnp.float32)
        * scale
    )
    token_pos = ctx_index * tok_dev + lax.iota(jnp.int32, tok_dev)
    key_pos = lax.iota(jnp.int32, resp_tokens)
    self_live = (key_pos[None, None, :] <= token_pos[:, None, None]) & (
        key_pos[None, None, :] < resp_len[None, :, None]
    )
    self_live = self_live[:, :, None, None, :]
    self_scores = jnp.where(self_live, self_scores, NEG_FILL)
    self_peak = jnp.max(self_scores, axis=-1)
    self_weights = jnp.where(self_live, jnp.exp(self_scores - self_peak[..., None]), 0.0)
    self_total = jnp.sum(self_weights, axis=-1)
    self_acc = jnp.einsum(
        "trgju,urgd->trgjd",
        self_weights.astype(jnp.bfloat16),
        fresh_values,
        preferred_element_type=jnp.float32,
    )
    flat = (row_count, kv_local, group)
    self_peak = self_peak.reshape(flat)
    self_total = self_total.reshape(flat)
    self_acc = self_acc.reshape(flat + (HEAD_SIZE,))

    remote_out = remote[:, :, 0]
    remote_lse = remote[:, :, 1]
    overall = jnp.maximum(jnp.max(remote_lse, axis=0), self_peak[..., None])
    remote_weight = jnp.exp(remote_lse - overall)
    self_factor = jnp.exp(self_peak[..., None] - overall)
    numerator = jnp.sum(remote_weight * remote_out, axis=0) + self_factor * self_acc
    denominator = jnp.sum(remote_weight, axis=0) + self_factor * self_total[..., None]
    result = numerator / denominator
    row_live = (token_pos[:, None] < resp_len[None, :]).reshape(row_count)
    result = jnp.where(row_live[:, None, None, None], result, 0.0)
    return result.reshape(tok_dev, 2, q_width).astype(jnp.bfloat16)


def solution(mesh):
    return jax.shard_map(
        shards,
        mesh=mesh,
        in_specs=(
            P(("pairs", "ctx"), None, None),
            P("ctx", "head"),
            P(None, "ctx", "head"),
            P("head"),
            P(None, "head"),
            P(None, ("pairs", "ctx"), "head"),
            P("pairs"),
            P("pairs"),
        ),
        out_specs=P(("pairs", "ctx"), None, "head"),
        check_vma=False,
    )
```

```python
import functools

import jax
import jax.numpy as jnp
from jax import lax
from jax.experimental import pallas as pl
from jax.experimental.pallas import tpu as pltpu
from jax.sharding import PartitionSpec as P

HEAD_SIZE = 128
NEG_FILL = -1e30
MIB = 2**20
STAT_ROWS = 16
PROJECT_LIMIT = 53 * MIB

ANY = pl.BlockSpec(memory_space=pl.ANY)
VMEM = pl.BlockSpec(memory_space=pltpu.VMEM)
SMEM = pl.BlockSpec(memory_space=pltpu.SMEM)


def project_kernel(pieces, rows_ref, wq, wkv, out_ref, wq_here, wkv_here, sems):
    width = wq.shape[1] // pieces
    k_width = wkv.shape[2]
    copies = [
        pltpu.make_async_copy(wq.at[:, pl.ds(i * width, width)], wq_here.at[i], sems.at[i])
        for i in range(pieces)
    ]
    copies += [
        pltpu.make_async_copy(wkv.at[i], wkv_here.at[i], sems.at[pieces + i]) for i in range(2)
    ]
    for copy in copies:
        copy.start()
    if len(rows_ref.shape) == 3:
        rows = jnp.concatenate([rows_ref[i] for i in range(rows_ref.shape[0])], axis=0)
    else:
        rows = rows_ref[...]
    for i in range(pieces):
        copies[i].wait()
        out_ref[:, i * width : (i + 1) * width] = jnp.dot(
            rows, wq_here[i], preferred_element_type=jnp.float32
        )
    for i in range(2):
        copies[pieces + i].wait()
        first = pieces * width + i * k_width
        out_ref[:, first : first + k_width] = jnp.dot(
            rows, wkv_here[i], preferred_element_type=jnp.float32
        )


def project(rows, wq, wkv, pieces):
    depth, q_width = wq.shape
    width = q_width + 2 * wkv.shape[2]
    return pl.pallas_call(
        functools.partial(project_kernel, pieces),
        out_shape=jax.ShapeDtypeStruct((rows.size // depth, width), jnp.float32),
        in_specs=[VMEM, ANY, ANY],
        out_specs=VMEM,
        scratch_shapes=[
            pltpu.VMEM((pieces, depth, q_width // pieces), wq.dtype),
            pltpu.VMEM(wkv.shape, wkv.dtype),
            pltpu.SemaphoreType.DMA((pieces + 2,)),
        ],
        compiler_params=pltpu.CompilerParams(vmem_limit_bytes=PROJECT_LIMIT),
        name="project",
    )(rows, wq, wkv)


def attend_kernel(kv_local, group, tok_dev, place, limits, query, fresh, cache, out):
    rows = fresh.shape[1]
    size = out.shape[0]
    own = query.shape[1] // size
    cache_len = cache.shape[1]
    scale = HEAD_SIZE ** (-0.5)
    first_slot = place[0] * cache_len
    first_row = place[0] * 2 * tok_dev
    long = (query.shape[1], cache_len)
    live = first_slot + lax.broadcasted_iota(jnp.int32, long, 1) < limits[0]
    short = (query.shape[1], rows)
    row = lax.broadcasted_iota(jnp.int32, short, 0) // group
    key = lax.broadcasted_iota(jnp.int32, short, 1)
    mine = (row >= first_row) & (row < first_row + 2 * tok_dev)
    filled = jnp.where(key % 2 == 0, limits[1], limits[2])
    seen = mine & (key % 2 == row % 2) & (key // 2 <= row // 2) & (key // 2 < filled)
    lane = lax.broadcasted_iota(jnp.int32, (own, HEAD_SIZE), 1)
    place_in_owner = lax.broadcasted_iota(jnp.int32, (own, HEAD_SIZE), 0)
    contract = (((1,), (1,)), ((), ()))
    stats = jnp.zeros((size, HEAD_SIZE), jnp.float32)
    for g in range(kv_local):
        heads = slice(g * HEAD_SIZE, (g + 1) * HEAD_SIZE)
        q = query[g]
        scores = scale * lax.dot_general(
            q, cache[0, :, heads], contract, preferred_element_type=jnp.float32
        )
        scores = jnp.where(live, scores, NEG_FILL)
        near = scale * lax.dot_general(
            q, fresh[0, :, heads], contract, preferred_element_type=jnp.float32
        )
        near = jnp.where(seen, near, NEG_FILL)
        peak = jnp.maximum(
            jnp.max(scores, axis=1, keepdims=True), jnp.max(near, axis=1, keepdims=True)
        )
        weights = jnp.where(live, jnp.exp(scores - peak), 0.0)
        near_weights = jnp.where(seen, jnp.exp(near - peak), 0.0)
        total = jnp.sum(weights, axis=1, keepdims=True) + jnp.sum(
            near_weights, axis=1, keepdims=True
        )
        acc = jnp.dot(
            weights.astype(jnp.bfloat16), cache[1, :, heads], preferred_element_type=jnp.float32
        )
        acc = acc + jnp.dot(
            near_weights.astype(jnp.bfloat16),
            fresh[1, :, heads],
            preferred_element_type=jnp.float32,
        )
        some = total > 0.0
        safe = jnp.where(some, total, 1.0)
        lse = jnp.where(some, peak + jnp.log(safe), NEG_FILL)
        mean = (acc / safe).astype(jnp.bfloat16)
        out[:, g * own : (g + 1) * own, :] = mean.reshape(size, own, HEAD_SIZE)
        spread = jnp.where(
            (lane == g * own + place_in_owner)[None],
            jnp.broadcast_to(lse, (size * own, HEAD_SIZE)).reshape(size, own, HEAD_SIZE),
            0.0,
        )
        stats = stats + jnp.sum(spread, axis=1)
    high = stats.astype(jnp.bfloat16)
    rest = stats - high.astype(jnp.float32)
    middle = rest.astype(jnp.bfloat16)
    low = rest - middle.astype(jnp.float32)
    which = lax.broadcasted_iota(jnp.int32, (size, STAT_ROWS, HEAD_SIZE), 1)
    terms = jnp.where(
        which == 0,
        high.astype(jnp.float32)[:, None, :],
        jnp.where(which == 1, middle.astype(jnp.float32)[:, None, :], low[:, None, :]),
    )
    out[:, kv_local * own :, :] = terms.astype(jnp.bfloat16)


def attend(place, limits, query, fresh, cache, size, group, tok_dev):
    kv_local = query.shape[0]
    own = query.shape[1] // size
    return pl.pallas_call(
        functools.partial(attend_kernel, kv_local, group, tok_dev),
        out_shape=jax.ShapeDtypeStruct(
            (size, kv_local * own + STAT_ROWS, HEAD_SIZE), jnp.bfloat16
        ),
        in_specs=[SMEM, SMEM, VMEM, VMEM, VMEM],
        out_specs=VMEM,
        compiler_params=pltpu.CompilerParams(
            vmem_limit_bytes=8 * MIB if query.shape[1] <= 512 else 48 * MIB
        ),
        name="attend",
    )(place, limits, query, fresh, cache)


def combine_kernel(kv_local, group, tok_dev, place, limits, parts, out):
    count = out.shape[0]
    own = count // kv_local
    stats = (
        parts[:, count, :].astype(jnp.float32)
        + parts[:, count + 1, :].astype(jnp.float32)
        + parts[:, count + 2, :].astype(jnp.float32)
    )
    peak = jnp.max(stats, axis=0, keepdims=True)
    weights = jnp.exp(stats - peak)
    weights = weights / jnp.sum(weights, axis=0, keepdims=True)
    lane = lax.broadcasted_iota(jnp.int32, (1, HEAD_SIZE), 1)
    row = (lane % own) // group
    filled = jnp.where(row % 2 == 0, limits[1], limits[2])
    weights = jnp.where(place[0] * tok_dev + row // 2 < filled, weights, 0.0)
    mask = lax.broadcasted_iota(jnp.int32, (count, HEAD_SIZE), 0) == lax.broadcasted_iota(
        jnp.int32, (count, HEAD_SIZE), 1
    )
    spread = jnp.where(mask[None], weights[:, None, :], 0.0)
    column = jnp.sum(spread, axis=2, keepdims=True)
    out[...] = jnp.sum(column * parts[:, :count, :].astype(jnp.float32), axis=0)


def combine(place, limits, parts, kv_local, group, tok_dev):
    count = parts.shape[1] - STAT_ROWS
    return pl.pallas_call(
        functools.partial(combine_kernel, kv_local, group, tok_dev),
        out_shape=jax.ShapeDtypeStruct((count, HEAD_SIZE), jnp.float32),
        in_specs=[SMEM, SMEM, VMEM],
        out_specs=VMEM,
        compiler_params=pltpu.CompilerParams(vmem_limit_bytes=8 * MIB),
        name="combine",
    )(place, limits, parts)


def sum_over(value, axis, size):
    bit = 1
    while bit < size:
        pairs = [(d, d ^ bit) for d in range(size)]
        other = lax.ppermute(value.astype(jnp.bfloat16), axis, pairs)
        value = value + other.astype(jnp.float32)
        bit *= 2
    return value


def shards(hidden, wq, wkv, bias_q, bias_kv, key_value_cache, prompt_len, resp_len):
    tok_dev = hidden.shape[0]
    size = lax.axis_size("ctx")
    ctx_index = lax.axis_index("ctx")
    q_width = wq.shape[1]
    k_width = wkv.shape[2]
    kv_local = k_width // HEAD_SIZE
    group = q_width // k_width
    row_count = 2 * tok_dev
    rows = row_count * size
    place = ctx_index.astype(jnp.int32).reshape(1)
    limits = jnp.concatenate((prompt_len, resp_len))

    sent = hidden.reshape(row_count, size, hidden.shape[2] // size)
    columns = lax.all_to_all(sent, "ctx", split_axis=1, concat_axis=1, tiled=True)
    columns = jnp.swapaxes(columns, 0, 1)
    if size > 16:
        columns = columns.reshape(rows, columns.shape[2])
    partial = project(columns, wq, wkv, 4)
    bias_all = jnp.concatenate((bias_q, bias_kv[0], bias_kv[1])).astype(jnp.float32)
    projected = (sum_over(partial, "ctx", size) + bias_all).astype(jnp.bfloat16)
    query = projected[:, :q_width].reshape(rows, kv_local, group, HEAD_SIZE)
    query = jnp.transpose(query, (1, 0, 2, 3)).reshape(kv_local, rows * group, HEAD_SIZE)
    fresh = jnp.stack(
        (projected[:, q_width : q_width + k_width], projected[:, q_width + k_width :])
    )
    parts = attend(place, limits, query, fresh, key_value_cache, size, group, tok_dev)
    parts = lax.all_to_all(parts, "ctx", split_axis=0, concat_axis=0, tiled=True)
    result = combine(place, limits, parts, kv_local, group, tok_dev)
    result = result.reshape(kv_local, row_count, group, HEAD_SIZE)
    result = jnp.transpose(result, (1, 0, 2, 3))
    return result.reshape(tok_dev, 2, q_width).astype(jnp.bfloat16)


def solution(mesh):
    return jax.shard_map(
        shards,
        mesh=mesh,
        in_specs=(
            P(("pairs", "ctx"), None, None),
            P("ctx", "head"),
            P(None, "ctx", "head"),
            P("head"),
            P(None, "head"),
            P(None, ("pairs", "ctx"), "head"),
            P("pairs"),
            P("pairs"),
        ),
        out_specs=P(("pairs", "ctx"), None, "head"),
        check_vma=False,
    )
```

```python
import functools

import jax
import jax.numpy as jnp
from jax import lax
from jax.experimental import pallas as pl
from jax.experimental.pallas import tpu as pltpu
from jax.sharding import PartitionSpec as P

HEAD_SIZE = 128
NEG_FILL = -1e30
MIB = 2**20
STAT_ROWS = 16
LOAD_LIMIT = 49 * MIB + 512 * 1024
KEEP_LIMIT = 53 * MIB

ANY = pl.BlockSpec(memory_space=pl.ANY)
VMEM = pl.BlockSpec(memory_space=pltpu.VMEM)
SMEM = pl.BlockSpec(memory_space=pltpu.SMEM)


def weight_copies(head, wq, wkv, wq_here, wkv_here, sems, pieces):
    width = wq_here.shape[1] // pieces
    first = pl.multiple_of(head * wq_here.shape[1], HEAD_SIZE)
    copies = [
        pltpu.make_async_copy(
            wq.at[:, pl.ds(first + i * width, width)],
            wq_here.at[:, pl.ds(i * width, width)],
            sems.at[i],
        )
        for i in range(pieces)
    ]
    first = pl.multiple_of(head * HEAD_SIZE, HEAD_SIZE)
    for i in range(2):
        copies.append(
            pltpu.make_async_copy(
                wkv.at[i, :, pl.ds(first, HEAD_SIZE)], wkv_here.at[i], sems.at[pieces + i]
            )
        )
    for copy in copies:
        copy.start()
    return copies


def load_kernel(pieces, head, wq, wkv, wq_here, wkv_here, sems):
    for copy in weight_copies(head[0], wq, wkv, wq_here, wkv_here, sems, pieces):
        copy.wait()


def load(head, wq, wkv, pieces):
    depth, q_width = wq.shape
    shapes = ((depth, q_width // 2), (2, depth, HEAD_SIZE))
    moved = depth * (q_width + wkv.shape[2] * 2)
    return pl.pallas_call(
        functools.partial(load_kernel, pieces),
        out_shape=[jax.ShapeDtypeStruct(shape, wq.dtype) for shape in shapes],
        in_specs=[SMEM, ANY, ANY],
        out_specs=[VMEM] * 2,
        scratch_shapes=[pltpu.SemaphoreType.DMA((pieces + 2,))],
        compiler_params=pltpu.CompilerParams(vmem_limit_bytes=LOAD_LIMIT),
        cost_estimate=pl.CostEstimate(flops=0, bytes_accessed=2 * moved, transcendentals=0),
        name="load",
    )(head, wq, wkv)


def gather_rows(rows_ref):
    if len(rows_ref.shape) == 3:
        return jnp.concatenate([rows_ref[i] for i in range(rows_ref.shape[0])], axis=0)
    return rows_ref[...]


def send_kernel(rows_ref, wq_ref, wkv_ref, out_ref):
    rows = gather_rows(rows_ref)
    first = 0
    for weights in (wq_ref, wkv_ref.at[0], wkv_ref.at[1]):
        width = weights.shape[1]
        out_ref[:, first : first + width] = jnp.dot(
            rows, weights[...], preferred_element_type=jnp.float32
        ).astype(jnp.bfloat16)
        first += width


def send_part(rows, wq_half, wkv_half):
    depth, q_width = wq_half.shape
    return pl.pallas_call(
        send_kernel,
        out_shape=jax.ShapeDtypeStruct(
            (rows.size // depth, q_width + 2 * HEAD_SIZE), jnp.bfloat16
        ),
        in_specs=[VMEM] * 3,
        out_specs=VMEM,
        compiler_params=pltpu.CompilerParams(vmem_limit_bytes=8 * MIB),
        name="send_part",
    )(rows, wq_half, wkv_half)


def keep_kernel(pieces, head, rows_ref, wq, wkv, out_ref, wq_here, wkv_here, sems):
    copies = weight_copies(head[0], wq, wkv, wq_here, wkv_here, sems, pieces)
    rows = gather_rows(rows_ref)
    q_width = wq_here.shape[1]
    width = q_width // pieces
    for i in range(pieces):
        copies[i].wait()
        out_ref[:, i * width : (i + 1) * width] = jnp.dot(
            rows, wq_here[:, i * width : (i + 1) * width], preferred_element_type=jnp.float32
        )
    for i in range(2):
        copies[pieces + i].wait()
        first = q_width + i * HEAD_SIZE
        out_ref[:, first : first + HEAD_SIZE] = jnp.dot(
            rows, wkv_here[i], preferred_element_type=jnp.float32
        )


def keep_part(head, rows, wq, wkv, pieces):
    depth, q_width = wq.shape
    half = q_width // 2
    count = rows.size // depth
    width = half + 2 * HEAD_SIZE
    return pl.pallas_call(
        functools.partial(keep_kernel, pieces),
        out_shape=jax.ShapeDtypeStruct((count, width), jnp.float32),
        in_specs=[SMEM, VMEM, ANY, ANY],
        out_specs=VMEM,
        scratch_shapes=[
            pltpu.VMEM((depth, half), wq.dtype),
            pltpu.VMEM((2, depth, HEAD_SIZE), wkv.dtype),
            pltpu.SemaphoreType.DMA((pieces + 2,)),
        ],
        compiler_params=pltpu.CompilerParams(vmem_limit_bytes=KEEP_LIMIT),
        cost_estimate=pl.CostEstimate(
            flops=2 * count * depth * width, bytes_accessed=2 * depth * width, transcendentals=0
        ),
        name="keep_part",
    )(head, rows, wq, wkv)


def attend_kernel(group, tok_dev, place, limits, query, fresh, cache, swapped, out):
    rows = fresh.shape[1]
    size = out.shape[0]
    own = query.shape[0] // size
    cache_len = cache.shape[1]
    scale = HEAD_SIZE ** (-0.5)
    here = place[0]
    head = lax.rem(here, 2)
    heads = pl.ds(pl.multiple_of(head * HEAD_SIZE, HEAD_SIZE), HEAD_SIZE)
    beside = here + 1 - 2 * head
    first_row = (here - head) * 2 * tok_dev
    q = query[...]
    contract = (((1,), (1,)), ((), ()))
    slot = lax.broadcasted_iota(jnp.int32, (query.shape[0], cache_len), 1)

    def scored(keys, first_slot):
        scores = scale * lax.dot_general(q, keys, contract, preferred_element_type=jnp.float32)
        return jnp.where(slot < limits[0] - first_slot, scores, NEG_FILL)

    near_shape = (query.shape[0], rows)
    row = lax.broadcasted_iota(jnp.int32, near_shape, 0) // group
    key = lax.broadcasted_iota(jnp.int32, near_shape, 1)
    filled = jnp.where(key % 2 == 0, limits[1], limits[2])
    seen = (
        (row >= first_row)
        & (row < first_row + 4 * tok_dev)
        & (key % 2 == row % 2)
        & (key // 2 <= row // 2)
        & (key // 2 < filled)
    )
    near = scale * lax.dot_general(q, fresh[0], contract, preferred_element_type=jnp.float32)
    parts = (
        (scored(cache[0, :, heads], here * cache_len), cache[1, :, heads]),
        (scored(swapped[0], beside * cache_len), swapped[1]),
        (jnp.where(seen, near, NEG_FILL), fresh[1]),
    )
    peak = functools.reduce(
        jnp.maximum, (jnp.max(scores, axis=1, keepdims=True) for scores, _ in parts)
    )
    base = jnp.maximum(peak, NEG_FILL / 10)
    total = jnp.zeros_like(peak)
    acc = jnp.zeros((query.shape[0], HEAD_SIZE), jnp.float32)
    for scores, values in parts:
        weights = jnp.exp(scores - base)
        total = total + jnp.sum(weights, axis=1, keepdims=True)
        acc = acc + jnp.dot(
            weights.astype(jnp.bfloat16), values, preferred_element_type=jnp.float32
        )
    some = total > 0.0
    safe = jnp.where(some, total, 1.0)
    lse = jnp.where(some, base + jnp.log(safe), NEG_FILL)
    out[:, :own, :] = (acc / safe).astype(jnp.bfloat16).reshape(size, own, HEAD_SIZE)
    lane = lax.broadcasted_iota(jnp.int32, (own, HEAD_SIZE), 1)
    line = lax.broadcasted_iota(jnp.int32, (own, HEAD_SIZE), 0)
    spread = jnp.broadcast_to(lse, (size * own, HEAD_SIZE)).reshape(size, own, HEAD_SIZE)
    stats = jnp.sum(jnp.where((lane == line)[None], spread, 0.0), axis=1)
    high = stats.astype(jnp.bfloat16).astype(jnp.float32)
    rest = stats - high
    middle = rest.astype(jnp.bfloat16).astype(jnp.float32)
    low = rest - middle
    which = lax.broadcasted_iota(jnp.int32, (size, STAT_ROWS, HEAD_SIZE), 1)
    terms = jnp.where(
        which == 0, high[:, None, :], jnp.where(which == 1, middle[:, None, :], low[:, None, :])
    )
    out[:, own:, :] = terms.astype(jnp.bfloat16)


def attend(place, limits, query, fresh, cache, swapped, size, group, tok_dev):
    own = query.shape[0] // size
    return pl.pallas_call(
        functools.partial(attend_kernel, group, tok_dev),
        out_shape=jax.ShapeDtypeStruct((size, own + STAT_ROWS, HEAD_SIZE), jnp.bfloat16),
        in_specs=[SMEM, SMEM, VMEM, VMEM, VMEM, VMEM],
        out_specs=VMEM,
        compiler_params=pltpu.CompilerParams(
            vmem_limit_bytes=8 * MIB if query.shape[0] <= 256 else 48 * MIB
        ),
        name="attend",
    )(place, limits, query, fresh, cache, swapped)


def combine_kernel(group, tok_dev, place, limits, parts, out):
    size = parts.shape[0]
    own = out.shape[1]
    stats = (
        parts[:, own, :].astype(jnp.float32)
        + parts[:, own + 1, :].astype(jnp.float32)
        + parts[:, own + 2, :].astype(jnp.float32)
    )
    odd = lax.broadcasted_iota(jnp.int32, stats.shape, 0) % 2 == 1
    peaks = [
        jnp.max(jnp.where(odd == bool(g), stats, 2 * NEG_FILL), axis=0, keepdims=True)
        for g in range(2)
    ]
    weights = jnp.exp(stats - jnp.where(odd, peaks[1], peaks[0]))
    totals = [
        jnp.sum(jnp.where(odd == bool(g), weights, 0.0), axis=0, keepdims=True) for g in range(2)
    ]
    weights = weights / jnp.where(odd, totals[1], totals[0])
    row = (lax.broadcasted_iota(jnp.int32, stats.shape, 1) % own) // group
    filled = jnp.where(row % 2 == 0, limits[1], limits[2])
    weights = jnp.where(place[0] * tok_dev + row // 2 < filled, weights, 0.0)
    mask = lax.broadcasted_iota(jnp.int32, (own, HEAD_SIZE), 0) == lax.broadcasted_iota(
        jnp.int32, (own, HEAD_SIZE), 1
    )
    column = jnp.sum(jnp.where(mask[None], weights[:, None, :], 0.0), axis=2, keepdims=True)
    scaled = column * parts[:, :own, :].astype(jnp.float32)
    out[...] = jnp.sum(scaled.reshape(size // 2, 2, own, HEAD_SIZE), axis=0)


def combine(place, limits, parts, group, tok_dev):
    own = parts.shape[1] - STAT_ROWS
    return pl.pallas_call(
        functools.partial(combine_kernel, group, tok_dev),
        out_shape=jax.ShapeDtypeStruct((2, own, HEAD_SIZE), jnp.float32),
        in_specs=[SMEM, SMEM, VMEM],
        out_specs=VMEM,
        compiler_params=pltpu.CompilerParams(vmem_limit_bytes=8 * MIB),
        name="combine",
    )(place, limits, parts)


def swap(value, axis, size, bit):
    return lax.ppermute(value, axis, [(d, d ^ bit) for d in range(size)])


def shards(hidden, wq, wkv, bias_q, bias_kv, key_value_cache, prompt_len, resp_len):
    tok_dev = hidden.shape[0]
    size = lax.axis_size("ctx")
    here = lax.axis_index("ctx").astype(jnp.int32)
    q_width = wq.shape[1]
    k_width = wkv.shape[2]
    group = q_width // k_width
    half = q_width // 2
    row_count = 2 * tok_dev
    rows = row_count * size
    if k_width != 2 * HEAD_SIZE or size & (size - 1) or size < 2:
        raise ValueError("unsupported shapes")
    place = here.reshape(1)
    head = here % 2
    limits = jnp.concatenate((prompt_len, resp_len))

    sent = hidden.reshape(row_count, size, hidden.shape[2] // size)
    columns = lax.all_to_all(sent, "ctx", split_axis=1, concat_axis=1, tiled=True)
    columns = jnp.swapaxes(columns, 0, 1)
    if size > 16:
        columns = columns.reshape(rows, columns.shape[2])

    other = (1 - head) * HEAD_SIZE
    swapped = swap(
        lax.dynamic_slice_in_dim(key_value_cache, other, HEAD_SIZE, 2), "ctx", size, 1
    )
    wq_half, wkv_half = load((1 - head).reshape(1), wq, wkv, 2)
    received = swap(send_part(columns, wq_half, wkv_half), "ctx", size, 1)
    kept = keep_part(head.reshape(1), columns, wq, wkv, 4)
    value = kept + received.astype(jnp.float32)
    bit = 2
    while bit < size:
        received = swap(value.astype(jnp.bfloat16), "ctx", size, bit)
        value = value + received.astype(jnp.float32)
        bit *= 2
    bias = jnp.concatenate(
        (
            lax.dynamic_slice_in_dim(bias_q, head * half, half),
            lax.dynamic_slice_in_dim(bias_kv, head * HEAD_SIZE, HEAD_SIZE, 1).reshape(-1),
        )
    ).astype(jnp.float32)
    projected = (value + bias).astype(jnp.bfloat16)
    query = projected[:, :half].reshape(rows * group, HEAD_SIZE)
    fresh = jnp.stack((projected[:, half : half + HEAD_SIZE], projected[:, half + HEAD_SIZE :]))
    parts = attend(place, limits, query, fresh, key_value_cache, swapped, size, group, tok_dev)
    parts = lax.all_to_all(parts, "ctx", split_axis=0, concat_axis=0, tiled=True)
    result = combine(place, limits, parts, group, tok_dev)
    result = result.reshape(2, row_count, group, HEAD_SIZE)
    result = jnp.transpose(result, (1, 0, 2, 3))
    return result.reshape(tok_dev, 2, q_width).astype(jnp.bfloat16)


def solution(mesh):
    return jax.shard_map(
        shards,
        mesh=mesh,
        in_specs=(
            P(("pairs", "ctx"), None, None),
            P("ctx", "head"),
            P(None, "ctx", "head"),
            P("head"),
            P(None, "head"),
            P(None, ("pairs", "ctx"), "head"),
            P("pairs"),
            P("pairs"),
        ),
        out_specs=P(("pairs", "ctx"), None, "head"),
        check_vma=False,
    )
```
